32 devices in a mesh: gx: 2 (over y), gy: 4 (over x, core), gz: 4 (over z).
Axes of the slice: x: 2, y: 2, z: 4, core: 2. Of those that a mesh axis runs over, the one named last changes fastest.
Arguments:
- volume: bfloat16 [32, 64, 32, 256], P('gx', 'gy', 'gz'), may hold values from -6 to 6
- offsets: int32 [2, 3], replicated, may hold values from 0 to 4, as said below
- coefficients: float32 [5], replicated, may hold values from -0.15 to 0.5
Outputs:
- denoised: bfloat16 [32, 64, 32, 256], P('gx', 'gy', 'gz')
The draws below stay inside these ranges and needn't reach their ends.
Inputs may be any that keep to these rules, and one draw needn't show every extreme that they name: `offsets`: every entry is 0 or 4; along each spatial dimension at least one of the passes has 4.
All inputs are finite; a program needn't handle non-finite values.
Results may differ from the reference program's by a relative error of at most 0.0062.
Values may be sent and summed in bfloat16 or wider, within the bound.
No kernel may reach another device: no remote copies, remote signals or barrier semaphores. Data moves between devices by JAX's collectives and lax.ppermute only.
A program may use at most 64 MiB of HBM per device.

```python
import jax
import jax.numpy as jnp
from jax import lax

FRAMES = 256
BLK = 8
PASSES = 2
SHIFT = 4
VOXB = 512
NX = 32
NY = 64
NZ = 32


def draw_offsets(key, part):
    pattern = jax.random.randint(key, (3,), 0, 3)
    leading = jnp.where(pattern != 1, SHIFT, 0)
    trailing = jnp.where(pattern != 0, SHIFT, 0)
    return jnp.stack([leading, trailing]).astype(jnp.int32)


def draw_coefficients(key, part):
    lower_end = jnp.array([0.2, 0.3, -0.15, 0.01, -0.004], jnp.float32)
    upper_end = jnp.array([0.4, 0.5, -0.05, 0.04, -0.001], jnp.float32)
    uniform_draw = jax.random.uniform(key, (5,), jnp.float32)
    return (lower_end + (upper_end - lower_end) * uniform_draw).astype(jnp.float32)


def shard_levels(rng, shape, cuts, low, largest):
    gain = 1.0
    for axis_at, blocks in cuts:
        draws = jax.random.uniform(jax.random.fold_in(jax.random.fold_in(rng, 6), axis_at), (blocks,), jnp.float32, low / len(cuts), largest / len(cuts))
        gain = gain * jnp.repeat(jnp.exp(draws), shape[axis_at] // blocks).reshape((-1,) + (1,) * (len(shape) - 1 - axis_at))
    return gain


def scatter_about(key, dims, spread, bound, shards=(), kind=jnp.bfloat16):
    entries = spread * jax.random.normal(key, dims, jnp.float32)
    if shards:
        entries = entries * shard_levels(key, dims, shards, -0.22, 0.18)
    return jnp.clip(entries, -bound, bound).astype(kind)


def setup_inputs(seed: int = 0) -> dict:
    key_list = jax.random.split(jax.random.key(seed), 4)
    volume = scatter_about(key_list[0], (NX, NY, NZ, FRAMES), 1.0, 6.0, ((0, 2), (1, 4), (2, 4)))
    offsets = draw_offsets(jax.random.fold_in(key_list[3], 71), 0)
    coefficients = draw_coefficients(jax.random.fold_in(key_list[3], 71), 0)
    return dict(volume=volume, offsets=offsets, coefficients=coefficients)


def to_blocks(volume_now):
    sizes = volume_now.shape
    shaped = volume_now.reshape(sizes[0] // BLK, BLK, sizes[1] // BLK, BLK, sizes[2] // BLK, BLK, sizes[3])
    return shaped.transpose(0, 2, 4, 1, 3, 5, 6).reshape(-1, VOXB, sizes[3])


def from_blocks(blocks, sizes):
    shaped = blocks.reshape(sizes[0] // BLK, sizes[1] // BLK, sizes[2] // BLK, BLK, BLK, BLK, sizes[3])
    return shaped.transpose(0, 3, 1, 4, 2, 5, 6).reshape(sizes)


def shrink(blocks, coefficients):
    highest = lax.Precision.HIGHEST
    wide = blocks.astype(jnp.float32)
    gramian = jnp.einsum('bvf,bvg->bfg', wide, wide, precision=highest)
    frames = gramian.shape[-1]
    voxels = blocks.shape[1]
    diag_mean = jnp.trace(gramian, axis1=1, axis2=2) / (voxels * frames)
    scaled = gramian / (voxels * (diag_mean + 1e-6))[:, None, None]
    identity = jnp.eye(frames, dtype=jnp.float32)
    poly = coefficients[4] * scaled + coefficients[3] * identity
    for degree_index in (2, 1, 0):
        poly = jnp.einsum('bfg,bgh->bfh', poly, scaled, precision=highest) + coefficients[degree_index] * identity
    poly_half = poly.astype(jnp.bfloat16).astype(jnp.float32)
    result = jnp.einsum('bvf,bfg->bvg', wide, poly_half, precision=highest)
    return result.astype(jnp.bfloat16)


def one_pass(volume_now, shifts, coefficients):
    rolled = volume_now
    for axis_index in range(3):
        rolled = jnp.roll(rolled, -shifts[axis_index], axis=axis_index)
    blocks = to_blocks(rolled)
    groups = blocks.reshape(-1, 16, VOXB, blocks.shape[2])
    finished = lax.map(lambda group: shrink(group, coefficients), groups)
    shrunk = from_blocks(finished.reshape(blocks.shape), rolled.shape)
    for axis_index in range(3):
        shrunk = jnp.roll(shrunk, shifts[axis_index], axis=axis_index)
    return shrunk


def reference(volume, offsets, coefficients):
    current = volume
    for pass_index in range(PASSES):
        current = one_pass(current, offsets[pass_index], coefficients)
    return current
```

```python
import itertools

import jax
import jax.numpy as jnp
from jax import lax
from jax.experimental import pallas as pl
from jax.experimental.pallas import tpu as pltpu
from jax.sharding import PartitionSpec as P

BLK = 8
SHIFT = 4
VOXB = 512
AXES = ("gx", "gy", "gz")
REGIONS = tuple(itertools.product((0, 1), repeat=3))


def slot_counts(shape):
    return tuple(size // SHIFT for size in shape[:3])


def region_shape(region, shape):
    nx, ny, nz = (1 if low else n - 1 for low, n in zip(region, slot_counts(shape)))
    return (nz, nx, SHIFT, ny, SHIFT * SHIFT, shape[3])


def region_slices(region):
    return tuple(slice(0, 1) if low else slice(1, None) for low in region)


def region_types(shape):
    return [jax.ShapeDtypeStruct(region_shape(region, shape), jnp.bfloat16) for region in REGIONS]


def split_kernel(shape, in_ref, *out_refs):
    nsx, nsy, nsz = slot_counts(shape)
    frames = shape[3]
    lower = lax.broadcasted_iota(jnp.int32, (shape[0], 2, 8, frames), 2) < SHIFT
    for zb in range(nsz // 2):
        for ys in range(nsy):
            part = in_ref[:, SHIFT * ys : SHIFT * (ys + 1), BLK * zb : BLK * (zb + 1), :].astype(jnp.float32)
            part = part.reshape(shape[0], 2, 2, 8, frames)
            first, second = part[:, :, 0], part[:, :, 1]
            halves = (
                jnp.where(lower, first, pltpu.roll(second, SHIFT, 2)),
                jnp.where(lower, pltpu.roll(first, SHIFT, 2), second),
            )
            for half, value in enumerate(halves):
                zs = 2 * zb + half
                value = value.reshape(nsx, SHIFT, 16, frames).astype(jnp.bfloat16)
                for region, out_ref in zip(REGIONS, out_refs):
                    if region[1] == (ys == 0) and region[2] == (zs == 0):
                        zi = 0 if region[2] else zs - 1
                        yi = 0 if region[1] else ys - 1
                        out_ref[zi, :, :, yi] = value[region_slices(region)[0]]


def split(volume):
    shape = volume.shape
    return pl.pallas_call(
        lambda *refs: split_kernel(shape, *refs),
        out_shape=region_types(shape),
        name="split",
    )(volume)


def merge_kernel(shape, *refs):
    out_ref = refs[-1]
    nsx, nsy, nsz = slot_counts(shape)
    frames = shape[3]
    lower = lax.broadcasted_iota(jnp.int32, (shape[0], 2, 8, frames), 2) < SHIFT
    for zb in range(nsz // 2):
        for ys in range(nsy):
            halves = []
            for zs in (2 * zb, 2 * zb + 1):
                pieces = []
                for low_x in (1, 0):
                    region = (low_x, int(ys == 0), int(zs == 0))
                    ref = refs[REGIONS.index(region)]
                    zi = 0 if region[2] else zs - 1
                    yi = 0 if region[1] else ys - 1
                    pieces.append(ref[zi, :, :, yi])
                value = jnp.concatenate(pieces, 0).astype(jnp.float32)
                halves.append(value.reshape(shape[0], 2, 8, frames))
            low, high = halves
            first = jnp.where(lower, low, pltpu.roll(high, SHIFT, 2))
            second = jnp.where(lower, pltpu.roll(low, SHIFT, 2), high)
            part = jnp.stack([first, second], 2).reshape(shape[0], SHIFT, 8, frames)
            out_ref[:, SHIFT * ys : SHIFT * (ys + 1), BLK * zb : BLK * (zb + 1), :] = part.astype(jnp.bfloat16)


def merge(regions, shape):
    return pl.pallas_call(
        lambda *refs: merge_kernel(shape, *refs),
        out_shape=jax.ShapeDtypeStruct(shape, jnp.bfloat16),
        name="merge",
    )(*regions)


def dot(a, b):
    return lax.dot_general(a, b, (((1,), (0,)), ((), ())), preferred_element_type=jnp.float32)


def halves_of(value):
    high = value.astype(jnp.bfloat16)
    return high, (value - high.astype(jnp.float32)).astype(jnp.bfloat16)


def wide_dot(a, b):
    (ah, al), (bh, bl) = a, b
    return dot(ah, bh) + (dot(ah, bl) + dot(al, bh))


def shrink_kernel(shape, pass_index, offsets_ref, coefficients_ref, *refs):
    in_refs, out_refs = refs[:8], refs[8:16]
    held, result, in_sems, out_sems = refs[16:]
    nsx, nsy, nsz = slot_counts(shape)
    frames = shape[3]

    def copies(to_scratch):
        made = []
        for at, region in enumerate(REGIONS):
            xsl, ysl, zsl = region_slices(region)
            scratch = (held if to_scratch else result).at[zsl, xsl, :, ysl]
            if to_scratch:
                made.append(pltpu.make_async_copy(in_refs[at], scratch, in_sems.at[at]))
            else:
                made.append(pltpu.make_async_copy(scratch, out_refs[at], out_sems.at[at]))
        return made

    arriving = copies(True)
    for copy in arriving:
        copy.start()
    moved = [offsets_ref[pass_index, dim] // SHIFT for dim in range(3)]
    c0, c1, c2, c3, c4 = (coefficients_ref[degree] for degree in range(5))
    rows = lax.broadcasted_iota(jnp.int32, (frames, frames), 0)
    columns = lax.broadcasted_iota(jnp.int32, (frames, frames), 1)
    on_diagonal = rows == columns
    for copy in arriving:
        copy.wait()
    for bz, bx, by in itertools.product(range(nsz // 2), range(nsx // 2), range(nsy // 2)):
        slots = []
        for first, count, shift in ((bz, nsz, moved[2]), (bx, nsx, moved[0]), (by, nsy, moved[1])):
            slots.append([lax.rem(2 * first + step + shift, count) for step in range(2)])
        chunks = list(itertools.product(*slots))
        block = jnp.concatenate(
            [held[zs, xs, :, ys].reshape(SHIFT * 16, frames) for zs, xs, ys in chunks], 0
        )
        gramian = lax.dot_general(
            block, block, (((0,), (0,)), ((), ())), preferred_element_type=jnp.float32
        )
        trace = jnp.sum(jnp.where(on_diagonal, gramian, 0.0))
        scaled = gramian * (1.0 / (VOXB * (trace / (VOXB * frames) + 1e-6)))
        narrow = halves_of(scaled)
        square = wide_dot(narrow, narrow)
        inner = c4 * square + c3 * scaled + jnp.where(on_diagonal, c2, 0.0)
        poly = wide_dot(halves_of(inner), halves_of(square)) + c1 * scaled + jnp.where(on_diagonal, c0, 0.0)
        rows_out = dot(block, poly.astype(jnp.bfloat16)).astype(jnp.bfloat16)
        for at, (zs, xs, ys) in enumerate(chunks):
            result[zs, xs, :, ys] = rows_out[64 * at : 64 * (at + 1)].reshape(SHIFT, 16, frames)
    leaving = copies(False)
    for copy in leaving:
        copy.start()
    for copy in leaving:
        copy.wait()


def shrink(regions, shape, pass_index, offsets, coefficients):
    nsx, nsy, nsz = slot_counts(shape)
    scratch = pltpu.VMEM((nsz, nsx, SHIFT, nsy, 16, shape[3]), jnp.bfloat16)
    whole = pl.BlockSpec(memory_space=pl.ANY)
    scalars = pl.BlockSpec(memory_space=pltpu.SMEM)
    return pl.pallas_call(
        lambda *refs: shrink_kernel(shape, pass_index, *refs),
        out_shape=region_types(shape),
        in_specs=[scalars, scalars] + [whole] * 8,
        out_specs=[whole] * 8,
        scratch_shapes=[scratch, scratch, pltpu.SemaphoreType.DMA((8,)), pltpu.SemaphoreType.DMA((8,))],
        name=f"shrink{pass_index}",
    )(offsets, coefficients, *regions)


def sent(value, steps):
    sizes = [lax.axis_size(axis) for axis in AXES]
    steps = [step % size for step, size in zip(steps, sizes)]
    if not any(steps):
        return value
    pairs = []
    for source, at in enumerate(itertools.product(*(range(size) for size in sizes))):
        target = 0
        for place, step, size in zip(at, steps, sizes):
            target = target * size + (place + step) % size
        pairs.append((source, target))
    return lax.ppermute(value, AXES, pairs)


def regroup(regions, step, choices):
    sizes = [lax.axis_size(axis) for axis in AXES]
    options = []
    index = 0
    for dim in range(3):
        kinds = {}
        for choice in choices:
            kinds.setdefault(choice % sizes[dim], []).append(choice)
        picked = 0
        for at, members in enumerate(kinds.values()):
            for member in members:
                picked = jnp.where(step[dim] == member, at, picked)
        index = index * len(kinds) + picked
        options.append(list(kinds))

    order = sorted(range(8), key=lambda at: (sum(REGIONS[at]), -REGIONS[at][2]))

    def branch(delta):
        def move(*held):
            out = list(held)
            for at in order:
                if any(REGIONS[at]):
                    out[at - 1] = sent(held[at - 1], [low * one for low, one in zip(REGIONS[at], delta)])
            return tuple(out)

        return move

    branches = [branch(delta) for delta in itertools.product(*options)]
    moved = lax.switch(index, branches, *regions[1:])
    return [regions[0], *moved]


def local(volume, offsets, coefficients):
    shape = volume.shape
    slots = offsets // SHIFT
    regions = split(volume)
    regions = regroup(regions, -slots[0], (0, -1))
    regions = shrink(regions, shape, 0, offsets, coefficients)
    regions = regroup(regions, slots[0] - slots[1], (0, -1, 1))
    regions = shrink(regions, shape, 1, offsets, coefficients)
    regions = regroup(regions, slots[1], (0, 1))
    return merge(regions, shape)


def solution(mesh):
    return jax.shard_map(
        local,
        mesh=mesh,
        in_specs=(P("gx", "gy", "gz", None), P(), P()),
        out_specs=P("gx", "gy", "gz", None),
        check_vma=False,
    )
```

```python
import itertools

import jax
import jax.numpy as jnp
from jax import lax
from jax.experimental import pallas as pl
from jax.experimental.pallas import tpu as pltpu
from jax.sharding import PartitionSpec as P

BLK = 8
SHIFT = 4
VOXB = 512
AXES = ("gx", "gy", "gz")
REGIONS = tuple(itertools.product((0, 1), repeat=3))


def slot_counts(shape):
    return tuple(size // SHIFT for size in shape[:3])


def region_shape(region, shape):
    nx, ny, nz = (1 if low else n - 1 for low, n in zip(region, slot_counts(shape)))
    return (nz, nx, SHIFT, ny, SHIFT * SHIFT, shape[3])


def region_slices(region):
    return tuple(slice(0, 1) if low else slice(1, None) for low in region)


def region_types(shape):
    return [jax.ShapeDtypeStruct(region_shape(region, shape), jnp.bfloat16) for region in REGIONS]


def groups(frames):
    return lax.broadcasted_iota(jnp.int32, (SHIFT, 16, frames), 1) % BLK < SHIFT


def pair_shape(shape):
    return (shape[0], shape[1] // 2, shape[2] // BLK, 2 * BLK, shape[3])


def split_kernel(shape, radices, offsets_ref, in_ref, *refs):
    out_refs, index_refs, (held, sems) = refs[:8], refs[8:11], refs[11:]
    nsx, nsy, nsz = slot_counts(shape)
    arriving = []
    for xs in range(nsx):
        part = pl.ds(SHIFT * xs, SHIFT)
        arriving.append(pltpu.make_async_copy(in_ref.at[part], held.at[part], sems.at[xs]))
        arriving[-1].start()
    for phase, index_ref in enumerate(index_refs):
        index = jnp.int32(0)
        for dim in range(3):
            before = offsets_ref[phase - 1, dim] // SHIFT if phase > 0 else 0
            after = offsets_ref[phase, dim] // SHIFT if phase < 2 else 0
            index = index * radices[phase][dim] + lax.rem(before - after + radices[phase][dim], radices[phase][dim])
        index_ref[0] = index
    lower = groups(shape[3])
    for xs in range(nsx):
        arriving[xs].wait()
        for ys, zb in itertools.product(range(nsy), range(nsz // 2)):
            first, second = (held[SHIFT * xs : SHIFT * (xs + 1), 2 * ys + at, zb] for at in range(2))
            halves = (
                jnp.where(lower, first, pltpu.roll(second, SHIFT, 1)),
                jnp.where(lower, pltpu.roll(first, 16 - SHIFT, 1), second),
            )
            for half, value in enumerate(halves):
                place, at = placed((xs, ys, 2 * zb + half))
                out_refs[place][at] = value


def placed(slot):
    region = tuple(int(one == 0) for one in slot)
    xi, yi, zi = (max(one - 1, 0) for one in slot)
    return REGIONS.index(region), (zi, xi, slice(None), yi)


def split(volume, offsets, radices):
    shape = volume.shape
    paired = pair_shape(shape)
    volume = volume.reshape(paired[0], paired[1], 2, paired[2], BLK, paired[4])
    volume = volume.transpose(0, 1, 3, 2, 4, 5).reshape(paired)
    nsx = slot_counts(shape)[0]
    made = pl.pallas_call(
        lambda *refs: split_kernel(shape, radices, *refs),
        out_shape=region_types(shape) + [jax.ShapeDtypeStruct((1,), jnp.int32)] * 3,
        in_specs=[pl.BlockSpec(memory_space=pltpu.SMEM), pl.BlockSpec(memory_space=pl.ANY)],
        out_specs=[pl.BlockSpec(memory_space=pltpu.VMEM)] * 8 + [pl.BlockSpec(memory_space=pltpu.SMEM)] * 3,
        scratch_shapes=[pltpu.VMEM(paired, jnp.bfloat16), pltpu.SemaphoreType.DMA((nsx,))],
        name="split",
    )(offsets, volume)
    return made[:8], [index[0] for index in made[8:]]


def merge_kernel(shape, *refs):
    in_refs, out_ref, held, sems = refs[:8], *refs[8:]
    nsx, nsy, nsz = slot_counts(shape)
    lower = groups(shape[3])
    leaving = []
    for xs in range(nsx):
        for ys, zb in itertools.product(range(nsy), range(nsz // 2)):
            halves = []
            for half in range(2):
                place, at = placed((xs, ys, 2 * zb + half))
                halves.append(in_refs[place][at])
            low, high = halves
            part = pl.ds(SHIFT * xs, SHIFT)
            held[part, 2 * ys, zb] = jnp.where(lower, low, pltpu.roll(high, SHIFT, 1))
            held[part, 2 * ys + 1, zb] = jnp.where(lower, pltpu.roll(low, 16 - SHIFT, 1), high)
        leaving.append(pltpu.make_async_copy(held.at[part], out_ref.at[part], sems.at[xs]))
        leaving[-1].start()
    for copy in leaving:
        copy.wait()


def merge(regions, shape):
    paired = pair_shape(shape)
    nsx = slot_counts(shape)[0]
    volume = pl.pallas_call(
        lambda *refs: merge_kernel(shape, *refs),
        out_shape=jax.ShapeDtypeStruct(paired, jnp.bfloat16),
        in_specs=[pl.BlockSpec(memory_space=pltpu.VMEM)] * 8,
        out_specs=pl.BlockSpec(memory_space=pl.ANY),
        scratch_shapes=[pltpu.VMEM(paired, jnp.bfloat16), pltpu.SemaphoreType.DMA((nsx,))],
        name="merge",
    )(*regions)
    volume = volume.reshape(paired[0], paired[1], paired[2], 2, BLK, paired[4])
    return volume.transpose(0, 1, 3, 2, 4, 5).reshape(shape)


def dot(a, b):
    return lax.dot_general(a, b, (((1,), (0,)), ((), ())), preferred_element_type=jnp.float32)


def halves_of(value):
    high = value.astype(jnp.bfloat16)
    return high, (value - high.astype(jnp.float32)).astype(jnp.bfloat16)


def wide_dot(a, b):
    (ah, al), (bh, bl) = a, b
    return dot(ah, bh) + (dot(ah, bl) + dot(al, bh))


def shrink_kernel(shape, pass_index, offsets_ref, coefficients_ref, *refs):
    in_refs, out_refs, (held, result) = refs[:8], refs[8:16], refs[16:]
    nsx, nsy, nsz = slot_counts(shape)
    frames = shape[3]
    for at, region in enumerate(REGIONS):
        xsl, ysl, zsl = region_slices(region)
        held[zsl, xsl, :, ysl] = in_refs[at][...]
    moved = [offsets_ref[pass_index, dim] // SHIFT for dim in range(3)]
    c0, c1, c2, c3, c4 = (coefficients_ref[degree] for degree in range(5))
    rows = lax.broadcasted_iota(jnp.int32, (frames, frames), 0)
    columns = lax.broadcasted_iota(jnp.int32, (frames, frames), 1)
    on_diagonal = rows == columns
    places = []
    for first in itertools.product(range(nsx // 2), range(nsy // 2), range(nsz // 2)):
        slots = [
            [lax.rem(2 * one + step + shift, count) for step in range(2)]
            for one, shift, count in zip(first, moved, (nsx, nsy, nsz))
        ]
        places.append(list(itertools.product(*slots)))

    def block_of(chunks):
        return jnp.concatenate([held[zs, xs, :, ys].reshape(SHIFT * 16, frames) for xs, ys, zs in chunks], 0)

    def scaled_gramian(block):
        gramian = lax.dot_general(
            block, block, (((0,), (0,)), ((), ())), preferred_element_type=jnp.float32
        )
        trace = jnp.sum(jnp.where(on_diagonal, gramian, 0.0))
        return gramian * (1.0 / (VOXB * (trace / (VOXB * frames) + 1e-6)))

    def squared(scaled):
        narrow = halves_of(scaled)
        return wide_dot(narrow, narrow)

    def polynomial(scaled, square):
        inner = c4 * square + c3 * scaled + jnp.where(on_diagonal, c2, 0.0)
        poly = wide_dot(halves_of(inner), halves_of(square)) + c1 * scaled + jnp.where(on_diagonal, c0, 0.0)
        return poly.astype(jnp.bfloat16)

    scaled = [scaled_gramian(block_of(chunks)) for chunks in places]
    squares = [squared(one) for one in scaled]
    polys = [polynomial(one, square) for one, square in zip(scaled, squares)]
    for chunks, poly in zip(places, polys):
        rows_out = dot(block_of(chunks), poly).astype(jnp.bfloat16)
        for at, (xs, ys, zs) in enumerate(chunks):
            result[zs, xs, :, ys] = rows_out[64 * at : 64 * (at + 1)].reshape(SHIFT, 16, frames)
    for at, region in enumerate(REGIONS):
        xsl, ysl, zsl = region_slices(region)
        out_refs[at][...] = result[zsl, xsl, :, ysl]


def shrink(regions, shape, pass_index, offsets, coefficients):
    nsx, nsy, nsz = slot_counts(shape)
    scratch = pltpu.VMEM((nsz, nsx, SHIFT, nsy, 16, shape[3]), jnp.bfloat16)
    whole = pl.BlockSpec(memory_space=pltpu.VMEM)
    scalars = pl.BlockSpec(memory_space=pltpu.SMEM)
    return pl.pallas_call(
        lambda *refs: shrink_kernel(shape, pass_index, *refs),
        out_shape=region_types(shape),
        in_specs=[scalars, scalars] + [whole] * 8,
        out_specs=[whole] * 8,
        scratch_shapes=[scratch, scratch],
        name=f"shrink{pass_index}",
    )(offsets, coefficients, *regions)


def sent(value, steps):
    sizes = [lax.axis_size(axis) for axis in AXES]
    steps = [step % size for step, size in zip(steps, sizes)]
    if not any(steps):
        return value
    pairs = []
    for source, at in enumerate(itertools.product(*(range(size) for size in sizes))):
        target = 0
        for place, step, size in zip(at, steps, sizes):
            target = target * size + (place + step) % size
        pairs.append((source, target))
    return lax.ppermute(value, AXES, pairs)


ORDER = ((0, 0, 1), (1, 0, 1), (0, 1, 1), (1, 1, 1), (1, 0, 0), (0, 1, 0), (1, 1, 0))


def regroup(regions, index, radices, way):
    def branch(delta):
        def move(*held):
            return tuple(
                sent(one, [low * step for low, step in zip(region, delta)]) for region, one in zip(ORDER, held)
            )

        return move

    steps = [[way * (digit if digit < 2 else digit - radix) for digit in range(radix)] for radix in radices]
    branches = [branch(delta) for delta in itertools.product(*steps)]
    moved = lax.switch(index, branches, *[regions[REGIONS.index(region)] for region in ORDER])
    moved = dict(zip(ORDER, moved))
    return [moved.get(region, regions[at]) for at, region in enumerate(REGIONS)]


def local(volume, offsets, coefficients):
    shape = volume.shape
    two_way = [2 if lax.axis_size(axis) == 2 else 3 for axis in AXES]
    radices = [(2, 2, 2), two_way, (2, 2, 2)]
    regions, index = split(volume, offsets, radices)
    regions = regroup(regions, index[0], radices[0], -1)
    regions = shrink(regions, shape, 0, offsets, coefficients)
    regions = regroup(regions, index[1], radices[1], 1)
    regions = shrink(regions, shape, 1, offsets, coefficients)
    regions = regroup(regions, index[2], radices[2], 1)
    return merge(regions, shape)


def solution(mesh):
    return jax.shard_map(
        local,
        mesh=mesh,
        in_specs=(P("gx", "gy", "gz", None), P(), P()),
        out_specs=P("gx", "gy", "gz", None),
        check_vma=False,
    )
```

```python
import itertools

import jax
import jax.numpy as jnp
from jax import lax
from jax._src.lax.control_flow import conditionals
from jax.experimental import pallas as pl
from jax.experimental.pallas import tpu as pltpu
from jax.sharding import PartitionSpec as P

BLK = 8
SHIFT = 4
VOXB = 512
AXES = ("gx", "gy", "gz")
REGIONS = tuple(itertools.product((0, 1), repeat=3))


def slot_counts(shape):
    return tuple(size // SHIFT for size in shape[:3])


def region_shape(region, shape):
    nx, ny, nz = (1 if low else n - 1 for low, n in zip(region, slot_counts(shape)))
    return (nz, nx, SHIFT, ny, SHIFT * SHIFT, shape[3])


def region_slices(region):
    return tuple(slice(0, 1) if low else slice(1, None) for low in region)


def region_types(shape):
    return [jax.ShapeDtypeStruct(region_shape(region, shape), jnp.bfloat16) for region in REGIONS]


def groups(frames):
    return lax.broadcasted_iota(jnp.int32, (SHIFT, 16, frames), 1) % BLK < SHIFT


def pair_shape(shape):
    return (shape[0], shape[1] // 2, shape[2] // BLK, 2 * BLK, shape[3])


def split_kernel(shape, radices, offsets_ref, coefficients_ref, in_ref, *refs):
    out_refs, index_refs, kept_refs, (held, sems) = refs[:8], refs[8:11], refs[11:13], refs[13:]
    nsx, nsy, nsz = slot_counts(shape)
    arriving = []
    for xs in range(nsx):
        part = pl.ds(SHIFT * xs, SHIFT)
        arriving.append(pltpu.make_async_copy(in_ref.at[part], held.at[part], sems.at[xs]))
        arriving[-1].start()
    for phase, index_ref in enumerate(index_refs):
        index = jnp.int32(0)
        for dim in range(3):
            before = offsets_ref[phase - 1, dim] // SHIFT if phase > 0 else 0
            after = offsets_ref[phase, dim] // SHIFT if phase < 2 else 0
            index = index * radices[phase][dim] + lax.rem(before - after + radices[phase][dim], radices[phase][dim])
        index_ref[0] = index
    for at in itertools.product(range(2), range(3)):
        kept_refs[0][at] = offsets_ref[at]
    for degree in range(5):
        kept_refs[1][degree] = coefficients_ref[degree]
    lower = groups(shape[3])
    for xs in range(nsx):
        arriving[xs].wait()
        for ys, zb in itertools.product(range(nsy), range(nsz // 2)):
            first, second = (held[SHIFT * xs : SHIFT * (xs + 1), 2 * ys + at, zb] for at in range(2))
            halves = (
                jnp.where(lower, first, pltpu.roll(second, SHIFT, 1)),
                jnp.where(lower, pltpu.roll(first, 16 - SHIFT, 1), second),
            )
            for half, value in enumerate(halves):
                place, at = placed((xs, ys, 2 * zb + half))
                out_refs[place][at] = value


def placed(slot):
    region = tuple(int(one == 0) for one in slot)
    xi, yi, zi = (max(one - 1, 0) for one in slot)
    return REGIONS.index(region), (zi, xi, slice(None), yi)


def split(volume, offsets, coefficients, radices):
    shape = volume.shape
    paired = pair_shape(shape)
    volume = volume.reshape(paired[0], paired[1], 2, paired[2], BLK, paired[4])
    volume = volume.transpose(0, 1, 3, 2, 4, 5).reshape(paired)
    nsx = slot_counts(shape)[0]
    made = pl.pallas_call(
        lambda *refs: split_kernel(shape, radices, *refs),
        out_shape=region_types(shape)
        + [pltpu.SMEM((1,), jnp.int32)] * 3
        + [pltpu.SMEM(offsets.shape, jnp.int32), pltpu.SMEM(coefficients.shape, jnp.float32)],
        in_specs=[pl.BlockSpec(memory_space=pltpu.SMEM)] * 2 + [pl.BlockSpec(memory_space=pl.ANY)],
        out_specs=[pl.BlockSpec(memory_space=pltpu.VMEM)] * 8 + [pl.BlockSpec(memory_space=pltpu.SMEM)] * 5,
        scratch_shapes=[pltpu.VMEM(paired, jnp.bfloat16), pltpu.SemaphoreType.DMA((nsx,))],
        name="split",
    )(offsets, coefficients, volume)
    return made[:8], [index[0] for index in made[8:11]], made[11], made[12]


def merge_kernel(shape, *refs):
    in_refs, out_ref, held, sems = refs[:8], *refs[8:]
    nsx, nsy, nsz = slot_counts(shape)
    lower = groups(shape[3])
    leaving = []
    for xs in range(nsx):
        for ys, zb in itertools.product(range(nsy), range(nsz // 2)):
            halves = []
            for half in range(2):
                place, at = placed((xs, ys, 2 * zb + half))
                halves.append(in_refs[place][at])
            low, high = halves
            part = pl.ds(SHIFT * xs, SHIFT)
            held[part, 2 * ys, zb] = jnp.where(lower, low, pltpu.roll(high, SHIFT, 1))
            held[part, 2 * ys + 1, zb] = jnp.where(lower, pltpu.roll(low, 16 - SHIFT, 1), high)
        leaving.append(pltpu.make_async_copy(held.at[part], out_ref.at[part], sems.at[xs]))
        leaving[-1].start()
    for copy in leaving:
        copy.wait()


def merge(regions, shape):
    paired = pair_shape(shape)
    nsx = slot_counts(shape)[0]
    volume = pl.pallas_call(
        lambda *refs: merge_kernel(shape, *refs),
        out_shape=jax.ShapeDtypeStruct(paired, jnp.bfloat16),
        in_specs=[pl.BlockSpec(memory_space=pltpu.VMEM)] * 8,
        out_specs=pl.BlockSpec(memory_space=pl.ANY),
        scratch_shapes=[pltpu.VMEM(paired, jnp.bfloat16), pltpu.SemaphoreType.DMA((nsx,))],
        name="merge",
    )(*regions)
    volume = volume.reshape(paired[0], paired[1], paired[2], 2, BLK, paired[4])
    return volume.transpose(0, 1, 3, 2, 4, 5).reshape(shape)


def dot(a, b):
    return lax.dot_general(a, b, (((1,), (0,)), ((), ())), preferred_element_type=jnp.float32)


def halves_of(value):
    high = value.astype(jnp.bfloat16)
    return high, (value - high.astype(jnp.float32)).astype(jnp.bfloat16)


def wide_dot(a, b):
    (ah, al), (bh, bl) = a, b
    return dot(ah, bh) + (dot(ah, bl) + dot(al, bh))


def shrink_kernel(shape, pass_index, offsets_ref, coefficients_ref, *refs):
    in_refs, out_refs, (held, result) = refs[:8], refs[8:16], refs[16:]
    nsx, nsy, nsz = slot_counts(shape)
    frames = shape[3]
    for at, region in enumerate(REGIONS):
        xsl, ysl, zsl = region_slices(region)
        held[zsl, xsl, :, ysl] = in_refs[at][...]
    moved = [offsets_ref[pass_index, dim] // SHIFT for dim in range(3)]
    c0, c1, c2, c3, c4 = (coefficients_ref[degree] for degree in range(5))
    rows = lax.broadcasted_iota(jnp.int32, (frames, frames), 0)
    columns = lax.broadcasted_iota(jnp.int32, (frames, frames), 1)
    on_diagonal = rows == columns
    places = []
    for first in itertools.product(range(nsx // 2), range(nsy // 2), range(nsz // 2)):
        slots = [
            [lax.rem(2 * one + step + shift, count) for step in range(2)]
            for one, shift, count in zip(first, moved, (nsx, nsy, nsz))
        ]
        places.append(list(itertools.product(*slots)))

    def block_of(chunks):
        return jnp.concatenate([held[zs, xs, :, ys].reshape(SHIFT * 16, frames) for xs, ys, zs in chunks], 0)

    def scaled_gramian(block):
        gramian = lax.dot_general(
            block, block, (((0,), (0,)), ((), ())), preferred_element_type=jnp.float32
        )
        trace = jnp.sum(jnp.where(on_diagonal, gramian, 0.0))
        return gramian * (1.0 / (VOXB * (trace / (VOXB * frames) + 1e-6)))

    def squared(scaled):
        narrow = halves_of(scaled)
        return wide_dot(narrow, narrow)

    def polynomial(scaled, square):
        inner = c4 * square + c3 * scaled + jnp.where(on_diagonal, c2, 0.0)
        poly = wide_dot(halves_of(inner), halves_of(square)) + c1 * scaled + jnp.where(on_diagonal, c0, 0.0)
        return poly.astype(jnp.bfloat16)

    scaled = [scaled_gramian(block_of(chunks)) for chunks in places]
    squares = [squared(one) for one in scaled]
    polys = [polynomial(one, square) for one, square in zip(scaled, squares)]
    for chunks, poly in zip(places, polys):
        rows_out = dot(block_of(chunks), poly).astype(jnp.bfloat16)
        for at, (xs, ys, zs) in enumerate(chunks):
            result[zs, xs, :, ys] = rows_out[64 * at : 64 * (at + 1)].reshape(SHIFT, 16, frames)
    for at, region in enumerate(REGIONS):
        xsl, ysl, zsl = region_slices(region)
        out_refs[at][...] = result[zsl, xsl, :, ysl]


def shrink(regions, shape, pass_index, offsets, coefficients):
    nsx, nsy, nsz = slot_counts(shape)
    scratch = pltpu.VMEM((nsz, nsx, SHIFT, nsy, 16, shape[3]), jnp.bfloat16)
    whole = pl.BlockSpec(memory_space=pltpu.VMEM)
    scalars = pl.BlockSpec(memory_space=pltpu.SMEM)
    return pl.pallas_call(
        lambda *refs: shrink_kernel(shape, pass_index, *refs),
        out_shape=region_types(shape),
        in_specs=[scalars, scalars] + [whole] * 8,
        out_specs=[whole] * 8,
        scratch_shapes=[scratch, scratch],
        name=f"shrink{pass_index}",
    )(offsets, coefficients, *regions)


def sent(value, steps):
    sizes = [lax.axis_size(axis) for axis in AXES]
    steps = [step % size for step, size in zip(steps, sizes)]
    if not any(steps):
        return value
    pairs = []
    for source, at in enumerate(itertools.product(*(range(size) for size in sizes))):
        target = 0
        for place, step, size in zip(at, steps, sizes):
            target = target * size + (place + step) % size
        pairs.append((source, target))
    return lax.ppermute(value, AXES, pairs)


ORDER = ((0, 0, 1), (1, 0, 1), (0, 1, 1), (1, 1, 1), (1, 0, 0), (0, 1, 0), (1, 1, 0), (0, 0, 0))


def regroup(regions, index, radices, way):
    def branch(delta):
        def move(*held):
            return tuple(
                sent(one, [low * step for low, step in zip(region, delta)])
                for region, one in zip(ORDER, held[:7])
            ) + (lax.optimization_barrier(held[7]),)

        return move

    steps = [[way * (digit if digit < 2 else digit - radix) for digit in range(radix)] for radix in radices]
    branches = [branch(delta) for delta in itertools.product(*steps)]
    operands = tuple(regions[REGIONS.index(region)] for region in ORDER)
    moved = conditionals._switch_internal(index, branches, operands, branches_platforms=None)
    moved = dict(zip(ORDER, moved))
    return [moved[region] for region in REGIONS]


def local(volume, offsets, coefficients):
    shape = volume.shape
    two_way = [2 if lax.axis_size(axis) == 2 else 3 for axis in AXES]
    radices = [(2, 2, 2), two_way, (2, 2, 2)]
    regions, index, offsets, coefficients = split(volume, offsets, coefficients, radices)
    regions = regroup(regions, index[0], radices[0], -1)
    regions = shrink(regions, shape, 0, offsets, coefficients)
    regions = regroup(regions, index[1], radices[1], 1)
    regions = shrink(regions, shape, 1, offsets, coefficients)
    regions = regroup(regions, index[2], radices[2], 1)
    return merge(regions, shape)


def solution(mesh):
    return jax.shard_map(
        local,
        mesh=mesh,
        in_specs=(P("gx", "gy", "gz", None), P(), P()),
        out_specs=P("gx", "gy", "gz", None),
        check_vma=False,
    )
```

```python
import itertools

import jax
import jax.numpy as jnp
from jax import lax
from jax._src.lax.control_flow import conditionals
from jax.experimental import pallas as pl
from jax.experimental.pallas import tpu as pltpu
from jax.sharding import PartitionSpec as P

BLK = 8
SHIFT = 4
VOXB = 512
AXES = ("gx", "gy", "gz")
MIRRORED = (0, 0, 1)
REGIONS = tuple(itertools.product((0, 1), repeat=3))


def slot_counts(shape):
    return tuple(size // SHIFT for size in shape[:3])


def region_shape(region, shape):
    nx, ny, nz = (1 if low else n - 1 for low, n in zip(region, slot_counts(shape)))
    return (nz, nx, SHIFT, ny, SHIFT * SHIFT, shape[3])


def region_slices(region, shape):
    slices = []
    for dim, (moves, count) in enumerate(zip(region, slot_counts(shape))):
        edge = count - 1 if MIRRORED[dim] else 0
        rest = (0, count - 1) if MIRRORED[dim] else (1, count)
        slices.append(slice(edge, edge + 1) if moves else slice(*rest))
    return tuple(slices)


def region_types(shape):
    return [jax.ShapeDtypeStruct(region_shape(region, shape), jnp.bfloat16) for region in REGIONS]


def groups(frames):
    return lax.broadcasted_iota(jnp.int32, (SHIFT, 16, frames), 1) % BLK < SHIFT


def pair_shape(shape):
    return (shape[0], shape[1] // 2, shape[2] // BLK, 2 * BLK, shape[3])


def split_kernel(shape, radices, offsets_ref, coefficients_ref, in_ref, *refs):
    out_refs, index_refs, kept_refs, (held, sems) = refs[:8], refs[8:11], refs[11:13], refs[13:]
    nsx, nsy, nsz = slot_counts(shape)
    arriving = []
    for xs in range(nsx):
        part = pl.ds(SHIFT * xs, SHIFT)
        arriving.append(pltpu.make_async_copy(in_ref.at[part], held.at[part], sems.at[xs]))
        arriving[-1].start()
    for phase, index_ref in enumerate(index_refs):
        index = jnp.int32(0)
        for dim in range(3):
            before = offsets_ref[phase - 1, dim] // SHIFT if phase > 0 else 0
            after = offsets_ref[phase, dim] // SHIFT if phase < 2 else 0
            index = index * radices[phase][dim] + lax.rem(before - after + radices[phase][dim], radices[phase][dim])
        index_ref[0] = index
    for at in itertools.product(range(2), range(3)):
        kept_refs[0][at] = offsets_ref[at]
    for degree in range(5):
        kept_refs[1][degree] = coefficients_ref[degree]
    lower = groups(shape[3])
    for xs in range(nsx):
        arriving[xs].wait()
        for ys, zb in itertools.product(range(nsy), range(nsz // 2)):
            first, second = (held[SHIFT * xs : SHIFT * (xs + 1), 2 * ys + at, zb] for at in range(2))
            halves = (
                jnp.where(lower, first, pltpu.roll(second, SHIFT, 1)),
                jnp.where(lower, pltpu.roll(first, 16 - SHIFT, 1), second),
            )
            for half, value in enumerate(halves):
                place, at = placed((xs, ys, 2 * zb + half), shape)
                out_refs[place][at] = value


def placed(slot, shape):
    region, at = [], []
    for dim, (one, count) in enumerate(zip(slot, slot_counts(shape))):
        moves = one == (count - 1 if MIRRORED[dim] else 0)
        region.append(int(moves))
        at.append(0 if moves else one - 1 + MIRRORED[dim])
    return REGIONS.index(tuple(region)), (at[2], at[0], slice(None), at[1])


def split(volume, offsets, coefficients, radices):
    shape = volume.shape
    paired = pair_shape(shape)
    volume = volume.reshape(paired[0], paired[1], 2, paired[2], BLK, paired[4])
    volume = volume.transpose(0, 1, 3, 2, 4, 5).reshape(paired)
    nsx = slot_counts(shape)[0]
    made = pl.pallas_call(
        lambda *refs: split_kernel(shape, radices, *refs),
        out_shape=region_types(shape)
        + [pltpu.SMEM((1,), jnp.int32)] * 3
        + [pltpu.SMEM(offsets.shape, jnp.int32), pltpu.SMEM(coefficients.shape, jnp.float32)],
        in_specs=[pl.BlockSpec(memory_space=pltpu.SMEM)] * 2 + [pl.BlockSpec(memory_space=pl.ANY)],
        out_specs=[pl.BlockSpec(memory_space=pltpu.VMEM)] * 8 + [pl.BlockSpec(memory_space=pltpu.SMEM)] * 5,
        scratch_shapes=[pltpu.VMEM(paired, jnp.bfloat16), pltpu.SemaphoreType.DMA((nsx,))],
        name="split",
    )(offsets, coefficients, volume)
    return made[:8], [index[0] for index in made[8:11]], made[11], made[12]


def merge_kernel(shape, *refs):
    in_refs, out_ref, held, sems = refs[:8], *refs[8:]
    nsx, nsy, nsz = slot_counts(shape)
    lower = groups(shape[3])
    leaving = []
    for xs in range(nsx):
        for ys, zb in itertools.product(range(nsy), range(nsz // 2)):
            halves = []
            for half in range(2):
                place, at = placed((xs, ys, 2 * zb + half), shape)
                halves.append(in_refs[place][at])
            low, high = halves
            part = pl.ds(SHIFT * xs, SHIFT)
            held[part, 2 * ys, zb] = jnp.where(lower, low, pltpu.roll(high, SHIFT, 1))
            held[part, 2 * ys + 1, zb] = jnp.where(lower, pltpu.roll(low, 16 - SHIFT, 1), high)
        leaving.append(pltpu.make_async_copy(held.at[part], out_ref.at[part], sems.at[xs]))
        leaving[-1].start()
    for copy in leaving:
        copy.wait()


def merge(regions, shape):
    paired = pair_shape(shape)
    nsx = slot_counts(shape)[0]
    volume = pl.pallas_call(
        lambda *refs: merge_kernel(shape, *refs),
        out_shape=jax.ShapeDtypeStruct(paired, jnp.bfloat16),
        in_specs=[pl.BlockSpec(memory_space=pltpu.VMEM)] * 8,
        out_specs=pl.BlockSpec(memory_space=pl.ANY),
        scratch_shapes=[pltpu.VMEM(paired, jnp.bfloat16), pltpu.SemaphoreType.DMA((nsx,))],
        name="merge",
    )(*regions)
    volume = volume.reshape(paired[0], paired[1], paired[2], 2, BLK, paired[4])
    return volume.transpose(0, 1, 3, 2, 4, 5).reshape(shape)


def dot(a, b):
    return lax.dot_general(a, b, (((1,), (0,)), ((), ())), preferred_element_type=jnp.float32)


def halves_of(value):
    high = value.astype(jnp.bfloat16)
    return high, (value - high.astype(jnp.float32)).astype(jnp.bfloat16)


def wide_dot(a, b):
    (ah, al), (bh, bl) = a, b
    return dot(ah, bh) + (dot(ah, bl) + dot(al, bh))


def shrink_kernel(shape, pass_index, offsets_ref, coefficients_ref, *refs):
    in_refs, out_refs, (held, result) = refs[:8], refs[8:16], refs[16:]
    nsx, nsy, nsz = slot_counts(shape)
    frames = shape[3]
    for at, region in enumerate(REGIONS):
        xsl, ysl, zsl = region_slices(region, shape)
        held[zsl, xsl, :, ysl] = in_refs[at][...]
    moved = [offsets_ref[pass_index, dim] // SHIFT for dim in range(3)]
    c0, c1, c2, c3, c4 = (coefficients_ref[degree] for degree in range(5))
    rows = lax.broadcasted_iota(jnp.int32, (frames, frames), 0)
    columns = lax.broadcasted_iota(jnp.int32, (frames, frames), 1)
    on_diagonal = rows == columns
    places = []
    for first in itertools.product(range(nsx // 2), range(nsy // 2), range(nsz // 2)):
        slots = [
            [lax.rem(2 * one + step + shift, count) for step in range(2)]
            for one, shift, count in zip(first, moved, (nsx, nsy, nsz))
        ]
        places.append(list(itertools.product(*slots)))

    def block_of(chunks):
        return jnp.concatenate([held[zs, xs, :, ys].reshape(SHIFT * 16, frames) for xs, ys, zs in chunks], 0)

    def scaled_gramian(block):
        gramian = lax.dot_general(
            block, block, (((0,), (0,)), ((), ())), preferred_element_type=jnp.float32
        )
        trace = jnp.sum(jnp.where(on_diagonal, gramian, 0.0))
        return gramian * (1.0 / (VOXB * (trace / (VOXB * frames) + 1e-6)))

    def squared(scaled):
        narrow = halves_of(scaled)
        return wide_dot(narrow, narrow)

    def polynomial(scaled, square):
        inner = c4 * square + c3 * scaled + jnp.where(on_diagonal, c2, 0.0)
        poly = wide_dot(halves_of(inner), halves_of(square)) + c1 * scaled + jnp.where(on_diagonal, c0, 0.0)
        return poly.astype(jnp.bfloat16)

    scaled = [scaled_gramian(block_of(chunks)) for chunks in places]
    squares = [squared(one) for one in scaled]
    polys = [polynomial(one, square) for one, square in zip(scaled, squares)]
    for chunks, poly in zip(places, polys):
        rows_out = dot(block_of(chunks), poly).astype(jnp.bfloat16)
        for at, (xs, ys, zs) in enumerate(chunks):
            result[zs, xs, :, ys] = rows_out[64 * at : 64 * (at + 1)].reshape(SHIFT, 16, frames)
    for at, region in enumerate(REGIONS):
        xsl, ysl, zsl = region_slices(region, shape)
        out_refs[at][...] = result[zsl, xsl, :, ysl]


def shrink(regions, shape, pass_index, offsets, coefficients):
    nsx, nsy, nsz = slot_counts(shape)
    scratch = pltpu.VMEM((nsz, nsx, SHIFT, nsy, 16, shape[3]), jnp.bfloat16)
    whole = pl.BlockSpec(memory_space=pltpu.VMEM)
    scalars = pl.BlockSpec(memory_space=pltpu.SMEM)
    return pl.pallas_call(
        lambda *refs: shrink_kernel(shape, pass_index, *refs),
        out_shape=region_types(shape),
        in_specs=[scalars, scalars] + [whole] * 8,
        out_specs=[whole] * 8,
        scratch_shapes=[scratch, scratch],
        name=f"shrink{pass_index}",
    )(offsets, coefficients, *regions)


def sent(value, steps):
    sizes = [lax.axis_size(axis) for axis in AXES]
    steps = [step % size for step, size in zip(steps, sizes)]
    if not any(steps):
        return value
    pairs = []
    for source, at in enumerate(itertools.product(*(range(size) for size in sizes))):
        target = 0
        for place, step, size in zip(at, steps, sizes):
            target = target * size + (place + step) % size
        pairs.append((source, target))
    return lax.ppermute(value, AXES, pairs)


ORDER = ((0, 0, 1), (1, 0, 1), (0, 1, 1), (1, 1, 1), (1, 0, 0), (0, 1, 0), (1, 1, 0), (0, 0, 0))


def regroup(regions, index, radices, way):
    def branch(delta):
        def move(*held):
            return tuple(
                sent(one, [moves * step * (-1 if other else 1) for moves, step, other in zip(region, delta, MIRRORED)])
                for region, one in zip(ORDER, held[:7])
            ) + (lax.optimization_barrier(held[7]),)

        return move

    steps = [[way * (digit if digit < 2 else digit - radix) for digit in range(radix)] for radix in radices]
    branches = [branch(delta) for delta in itertools.product(*steps)]
    operands = tuple(regions[REGIONS.index(region)] for region in ORDER)
    moved = conditionals._switch_internal(index, branches, operands, branches_platforms=None)
    moved = dict(zip(ORDER, moved))
    return [moved[region] for region in REGIONS]


def local(volume, offsets, coefficients):
    shape = volume.shape
    two_way = [2 if lax.axis_size(axis) == 2 else 3 for axis in AXES]
    radices = [(2, 2, 2), two_way, (2, 2, 2)]
    regions, index, offsets, coefficients = split(volume, offsets, coefficients, radices)
    regions = regroup(regions, index[0], radices[0], -1)
    regions = shrink(regions, shape, 0, offsets, coefficients)
    regions = regroup(regions, index[1], radices[1], 1)
    regions = shrink(regions, shape, 1, offsets, coefficients)
    regions = regroup(regions, index[2], radices[2], 1)
    return merge(regions, shape)


def solution(mesh):
    return jax.shard_map(
        local,
        mesh=mesh,
        in_specs=(P("gx", "gy", "gz", None), P(), P()),
        out_specs=P("gx", "gy", "gz", None),
        check_vma=False,
    )
```

```python
import itertools

import jax
import jax.numpy as jnp
from jax import lax
from jax._src.lax.control_flow import conditionals
from jax.experimental import pallas as pl
from jax.experimental.pallas import tpu as pltpu
from jax.sharding import PartitionSpec as P

BLK = 8
SHIFT = 4
VOXB = 512
AXES = ("gx", "gy", "gz")
MIRRORED = (0, 0, 1)
REGIONS = tuple(itertools.product((0, 1), repeat=3))


def slot_counts(shape):
    return tuple(size // SHIFT for size in shape[:3])


def region_shape(region, shape):
    nx, ny, nz = (1 if low else n - 1 for low, n in zip(region, slot_counts(shape)))
    return (nz, nx, SHIFT, ny, SHIFT * SHIFT, shape[3])


def region_slices(region, shape):
    slices = []
    for dim, (moves, count) in enumerate(zip(region, slot_counts(shape))):
        edge = count - 1 if MIRRORED[dim] else 0
        rest = (0, count - 1) if MIRRORED[dim] else (1, count)
        slices.append(slice(edge, edge + 1) if moves else slice(*rest))
    return tuple(slices)


def region_types(shape):
    return [jax.ShapeDtypeStruct(region_shape(region, shape), jnp.bfloat16) for region in REGIONS]


def groups(frames):
    return lax.broadcasted_iota(jnp.int32, (SHIFT, 16, frames), 1) % BLK < SHIFT


def pair_shape(shape):
    return (shape[0], shape[1] // 2, shape[2] // BLK, 2 * BLK, shape[3])


def split_kernel(shape, radices, offsets_ref, coefficients_ref, in_ref, *refs):
    out_refs, index_refs, kept_refs, (held, sems, kept_sems) = refs[:8], refs[8:11], refs[11:13], refs[13:]
    nsx, nsy, nsz = slot_counts(shape)
    arriving = []
    for xs in range(nsx):
        part = pl.ds(SHIFT * xs, SHIFT)
        arriving.append(pltpu.make_async_copy(in_ref.at[part], held.at[part], sems.at[xs]))
        arriving[-1].start()
    keeping = [
        pltpu.make_async_copy(ref, kept_refs[at], kept_sems.at[at])
        for at, ref in enumerate((offsets_ref, coefficients_ref))
    ]
    for copy in keeping:
        copy.start()
    for copy in keeping:
        copy.wait()
    offsets_ref = kept_refs[0]
    for phase, index_ref in enumerate(index_refs):
        index = jnp.int32(0)
        for dim in range(3):
            before = offsets_ref[phase - 1, dim] // SHIFT if phase > 0 else 0
            after = offsets_ref[phase, dim] // SHIFT if phase < 2 else 0
            index = index * radices[phase][dim] + lax.rem(before - after + radices[phase][dim], radices[phase][dim])
        index_ref[0] = index
    lower = groups(shape[3])
    for xs in range(nsx):
        arriving[xs].wait()
        for ys, zb in itertools.product(range(nsy), range(nsz // 2)):
            first, second = (held[SHIFT * xs : SHIFT * (xs + 1), 2 * ys + at, zb] for at in range(2))
            halves = (
                jnp.where(lower, first, pltpu.roll(second, SHIFT, 1)),
                jnp.where(lower, pltpu.roll(first, 16 - SHIFT, 1), second),
            )
            for half, value in enumerate(halves):
                place, at = placed((xs, ys, 2 * zb + half), shape)
                out_refs[place][at] = value


def placed(slot, shape):
    region, at = [], []
    for dim, (one, count) in enumerate(zip(slot, slot_counts(shape))):
        moves = one == (count - 1 if MIRRORED[dim] else 0)
        region.append(int(moves))
        at.append(0 if moves else one - 1 + MIRRORED[dim])
    return REGIONS.index(tuple(region)), (at[2], at[0], slice(None), at[1])


def split(volume, offsets, coefficients, radices):
    shape = volume.shape
    paired = pair_shape(shape)
    volume = volume.reshape(paired[0], paired[1], 2, paired[2], BLK, paired[4])
    volume = volume.transpose(0, 1, 3, 2, 4, 5).reshape(paired)
    nsx = slot_counts(shape)[0]
    made = pl.pallas_call(
        lambda *refs: split_kernel(shape, radices, *refs),
        out_shape=region_types(shape)
        + [pltpu.SMEM((1,), jnp.int32)] * 3
        + [pltpu.SMEM(offsets.shape, jnp.int32), pltpu.SMEM(coefficients.shape, jnp.float32)],
        in_specs=[pl.BlockSpec(memory_space=pl.ANY)] * 3,
        out_specs=[pl.BlockSpec(memory_space=pltpu.VMEM)] * 8 + [pl.BlockSpec(memory_space=pltpu.SMEM)] * 5,
        scratch_shapes=[
            pltpu.VMEM(paired, jnp.bfloat16),
            pltpu.SemaphoreType.DMA((nsx,)),
            pltpu.SemaphoreType.DMA((2,)),
        ],
        name="split",
    )(offsets, coefficients, volume)
    return made[:8], [index[0] for index in made[8:11]], made[11], made[12]


def merge_kernel(shape, *refs):
    in_refs, out_ref, held, sems = refs[:8], *refs[8:]
    nsx, nsy, nsz = slot_counts(shape)
    lower = groups(shape[3])
    leaving = []
    for xs in range(nsx):
        for ys, zb in itertools.product(range(nsy), range(nsz // 2)):
            halves = []
            for half in range(2):
                place, at = placed((xs, ys, 2 * zb + half), shape)
                halves.append(in_refs[place][at])
            low, high = halves
            part = pl.ds(SHIFT * xs, SHIFT)
            held[part, 2 * ys, zb] = jnp.where(lower, low, pltpu.roll(high, SHIFT, 1))
            held[part, 2 * ys + 1, zb] = jnp.where(lower, pltpu.roll(low, 16 - SHIFT, 1), high)
        leaving.append(pltpu.make_async_copy(held.at[part], out_ref.at[part], sems.at[xs]))
        leaving[-1].start()
    for copy in leaving:
        copy.wait()


def merge(regions, shape):
    paired = pair_shape(shape)
    nsx = slot_counts(shape)[0]
    volume = pl.pallas_call(
        lambda *refs: merge_kernel(shape, *refs),
        out_shape=jax.ShapeDtypeStruct(paired, jnp.bfloat16),
        in_specs=[pl.BlockSpec(memory_space=pltpu.VMEM)] * 8,
        out_specs=pl.BlockSpec(memory_space=pl.ANY),
        scratch_shapes=[pltpu.VMEM(paired, jnp.bfloat16), pltpu.SemaphoreType.DMA((nsx,))],
        name="merge",
    )(*regions)
    volume = volume.reshape(paired[0], paired[1], paired[2], 2, BLK, paired[4])
    return volume.transpose(0, 1, 3, 2, 4, 5).reshape(shape)


def dot(a, b):
    return lax.dot_general(a, b, (((1,), (0,)), ((), ())), preferred_element_type=jnp.float32)


def halves_of(value):
    high = value.astype(jnp.bfloat16)
    return high, (value - high.astype(jnp.float32)).astype(jnp.bfloat16)


def wide_dot(a, b):
    (ah, al), (bh, bl) = a, b
    return dot(ah, bh) + (dot(ah, bl) + dot(al, bh))


def shrink_kernel(shape, pass_index, offsets_ref, coefficients_ref, *refs):
    in_refs, out_refs, (held, result) = refs[:8], refs[8:16], refs[16:]
    nsx, nsy, nsz = slot_counts(shape)
    frames = shape[3]
    for at, region in enumerate(REGIONS):
        xsl, ysl, zsl = region_slices(region, shape)
        held[zsl, xsl, :, ysl] = in_refs[at][...]
    moved = [offsets_ref[pass_index, dim] // SHIFT for dim in range(3)]
    c0, c1, c2, c3, c4 = (coefficients_ref[degree] for degree in range(5))
    rows = lax.broadcasted_iota(jnp.int32, (frames, frames), 0)
    columns = lax.broadcasted_iota(jnp.int32, (frames, frames), 1)
    on_diagonal = rows == columns
    places = []
    for first in itertools.product(range(nsx // 2), range(nsy // 2), range(nsz // 2)):
        slots = [
            [lax.rem(2 * one + step + shift, count) for step in range(2)]
            for one, shift, count in zip(first, moved, (nsx, nsy, nsz))
        ]
        places.append(list(itertools.product(*slots)))

    def block_of(chunks):
        return jnp.concatenate([held[zs, xs, :, ys].reshape(SHIFT * 16, frames) for xs, ys, zs in chunks], 0)

    def scaled_gramian(block):
        gramian = lax.dot_general(
            block, block, (((0,), (0,)), ((), ())), preferred_element_type=jnp.float32
        )
        trace = jnp.sum(jnp.where(on_diagonal, gramian, 0.0))
        return gramian * (1.0 / (VOXB * (trace / (VOXB * frames) + 1e-6)))

    def squared(scaled):
        narrow = halves_of(scaled)
        return wide_dot(narrow, narrow)

    def polynomial(scaled, square):
        inner = c4 * square + c3 * scaled + jnp.where(on_diagonal, c2, 0.0)
        poly = wide_dot(halves_of(inner), halves_of(square)) + c1 * scaled + jnp.where(on_diagonal, c0, 0.0)
        return poly.astype(jnp.bfloat16)

    scaled = [scaled_gramian(block_of(chunks)) for chunks in places]
    squares = [squared(one) for one in scaled]
    polys = [polynomial(one, square) for one, square in zip(scaled, squares)]
    for chunks, poly in zip(places, polys):
        rows_out = dot(block_of(chunks), poly).astype(jnp.bfloat16)
        for at, (xs, ys, zs) in enumerate(chunks):
            result[zs, xs, :, ys] = rows_out[64 * at : 64 * (at + 1)].reshape(SHIFT, 16, frames)
    for at, region in enumerate(REGIONS):
        xsl, ysl, zsl = region_slices(region, shape)
        out_refs[at][...] = result[zsl, xsl, :, ysl]


def shrink(regions, shape, pass_index, offsets, coefficients):
    nsx, nsy, nsz = slot_counts(shape)
    scratch = pltpu.VMEM((nsz, nsx, SHIFT, nsy, 16, shape[3]), jnp.bfloat16)
    whole = pl.BlockSpec(memory_space=pltpu.VMEM)
    scalars = pl.BlockSpec(memory_space=pltpu.SMEM)
    return pl.pallas_call(
        lambda *refs: shrink_kernel(shape, pass_index, *refs),
        out_shape=region_types(shape),
        in_specs=[scalars, scalars] + [whole] * 8,
        out_specs=[whole] * 8,
        scratch_shapes=[scratch, scratch],
        name=f"shrink{pass_index}",
    )(offsets, coefficients, *regions)


def sent(value, steps):
    sizes = [lax.axis_size(axis) for axis in AXES]
    steps = [step % size for step, size in zip(steps, sizes)]
    if not any(steps):
        return value
    pairs = []
    for source, at in enumerate(itertools.product(*(range(size) for size in sizes))):
        target = 0
        for place, step, size in zip(at, steps, sizes):
            target = target * size + (place + step) % size
        pairs.append((source, target))
    return lax.ppermute(value, AXES, pairs)


ORDER = ((0, 0, 1), (1, 0, 1), (0, 1, 1), (1, 1, 1), (1, 0, 0), (0, 1, 0), (1, 1, 0), (0, 0, 0))


def regroup(regions, index, radices, way):
    def branch(delta):
        def move(*held):
            return tuple(
                sent(one, [moves * step * (-1 if other else 1) for moves, step, other in zip(region, delta, MIRRORED)])
                for region, one in zip(ORDER, held[:7])
            ) + (lax.optimization_barrier(held[7]),)

        return move

    steps = [[way * (digit if digit < 2 else digit - radix) for digit in range(radix)] for radix in radices]
    branches = [branch(delta) for delta in itertools.product(*steps)]
    operands = tuple(regions[REGIONS.index(region)] for region in ORDER)
    moved = conditionals._switch_internal(index, branches, operands, branches_platforms=None)
    moved = dict(zip(ORDER, moved))
    return [moved[region] for region in REGIONS]


def local(volume, offsets, coefficients):
    shape = volume.shape
    two_way = [2 if lax.axis_size(axis) == 2 else 3 for axis in AXES]
    radices = [(2, 2, 2), two_way, (2, 2, 2)]
    regions, index, offsets, coefficients = split(volume, offsets, coefficients, radices)
    regions = regroup(regions, index[0], radices[0], -1)
    regions = shrink(regions, shape, 0, offsets, coefficients)
    regions = regroup(regions, index[1], radices[1], 1)
    regions = shrink(regions, shape, 1, offsets, coefficients)
    regions = regroup(regions, index[2], radices[2], 1)
    return merge(regions, shape)


def solution(mesh):
    return jax.shard_map(
        local,
        mesh=mesh,
        in_specs=(P("gx", "gy", "gz", None), P(), P()),
        out_specs=P("gx", "gy", "gz", None),
        check_vma=False,
    )
```

```python
import itertools

import jax
import jax.numpy as jnp
from jax import lax
from jax._src.lax.control_flow import conditionals
from jax.experimental import pallas as pl
from jax.experimental.pallas import tpu as pltpu
from jax.sharding import PartitionSpec as P

BLK = 8
SHIFT = 4
VOXB = 512
AXES = ("gx", "gy", "gz")
MIRRORED = (0, 0, 1)
REGIONS = tuple(itertools.product((0, 1), repeat=3))


def slot_counts(shape):
    return tuple(size // SHIFT for size in shape[:3])


def region_shape(region, shape):
    nx, ny, nz = (1 if low else n - 1 for low, n in zip(region, slot_counts(shape)))
    return (nz, nx, SHIFT, ny, SHIFT * SHIFT, shape[3])


def region_slices(region, shape):
    slices = []
    for dim, (moves, count) in enumerate(zip(region, slot_counts(shape))):
        edge = count - 1 if MIRRORED[dim] else 0
        rest = (0, count - 1) if MIRRORED[dim] else (1, count)
        slices.append(slice(edge, edge + 1) if moves else slice(*rest))
    return tuple(slices)


def region_types(shape):
    return [jax.ShapeDtypeStruct(region_shape(region, shape), jnp.bfloat16) for region in REGIONS]


def groups(frames):
    return lax.broadcasted_iota(jnp.int32, (SHIFT, 16, frames), 1) % BLK < SHIFT


def pair_shape(shape):
    return (shape[0], shape[1] // 2, shape[2] // BLK, 2 * BLK, shape[3])


def split_kernel(shape, radices, offsets_ref, coefficients_ref, in_ref, *refs):
    out_refs, index_refs, kept_refs, (held, sems, kept_sems) = refs[:8], refs[8:11], refs[11:13], refs[13:]
    nsx, nsy, nsz = slot_counts(shape)
    arriving = []
    for xs in range(nsx):
        part = pl.ds(SHIFT * xs, SHIFT)
        arriving.append(pltpu.make_async_copy(in_ref.at[part], held.at[part], sems.at[xs]))
        arriving[-1].start()
    keeping = [
        pltpu.make_async_copy(ref, kept_refs[at], kept_sems.at[at])
        for at, ref in enumerate((offsets_ref, coefficients_ref))
    ]
    for copy in keeping:
        copy.start()
    for copy in keeping:
        copy.wait()
    offsets_ref = kept_refs[0]
    for phase, index_ref in enumerate(index_refs):
        index = jnp.int32(0)
        for dim in range(3):
            before = offsets_ref[phase - 1, dim] // SHIFT if phase > 0 else 0
            after = offsets_ref[phase, dim] // SHIFT if phase < 2 else 0
            index = index * radices[phase][dim] + lax.rem(before - after + radices[phase][dim], radices[phase][dim])
        index_ref[0] = index
    lower = groups(shape[3])
    for xs in range(nsx):
        arriving[xs].wait()
        for ys, zb in itertools.product(range(nsy), range(nsz // 2)):
            first, second = (held[SHIFT * xs : SHIFT * (xs + 1), 2 * ys + at, zb] for at in range(2))
            halves = (
                jnp.where(lower, first, pltpu.roll(second, SHIFT, 1)),
                jnp.where(lower, pltpu.roll(first, 16 - SHIFT, 1), second),
            )
            for half, value in enumerate(halves):
                place, at = placed((xs, ys, 2 * zb + half), shape)
                out_refs[place][at] = value


def placed(slot, shape):
    region, at = [], []
    for dim, (one, count) in enumerate(zip(slot, slot_counts(shape))):
        moves = one == (count - 1 if MIRRORED[dim] else 0)
        region.append(int(moves))
        at.append(0 if moves else one - 1 + MIRRORED[dim])
    return REGIONS.index(tuple(region)), (at[2], at[0], slice(None), at[1])


def split(volume, offsets, coefficients, radices):
    shape = volume.shape
    paired = pair_shape(shape)
    volume = volume.reshape(paired[0], paired[1], 2, paired[2], BLK, paired[4])
    volume = volume.transpose(0, 1, 3, 2, 4, 5).reshape(paired)
    nsx = slot_counts(shape)[0]
    made = pl.pallas_call(
        lambda *refs: split_kernel(shape, radices, *refs),
        out_shape=region_types(shape)
        + [pltpu.SMEM((1,), jnp.int32)] * 3
        + [pltpu.SMEM(offsets.shape, jnp.int32), pltpu.SMEM(coefficients.shape, jnp.float32)],
        in_specs=[pl.BlockSpec(memory_space=pl.ANY)] * 3,
        out_specs=[pl.BlockSpec(memory_space=pltpu.VMEM)] * 8 + [pl.BlockSpec(memory_space=pltpu.SMEM)] * 5,
        scratch_shapes=[
            pltpu.VMEM(paired, jnp.bfloat16),
            pltpu.SemaphoreType.DMA((nsx,)),
            pltpu.SemaphoreType.DMA((2,)),
        ],
        name="split",
    )(offsets, coefficients, volume)
    return made[:8], [index[0] for index in made[8:11]], made[11], made[12]


def merge_kernel(shape, *refs):
    in_refs, out_ref, held, sems = refs[:8], *refs[8:]
    nsx, nsy, nsz = slot_counts(shape)
    lower = groups(shape[3])
    leaving = []
    for xs in range(nsx):
        for ys, zb in itertools.product(range(nsy), range(nsz // 2)):
            halves = []
            for half in range(2):
                place, at = placed((xs, ys, 2 * zb + half), shape)
                halves.append(in_refs[place][at])
            low, high = halves
            part = pl.ds(SHIFT * xs, SHIFT)
            held[part, 2 * ys, zb] = jnp.where(lower, low, pltpu.roll(high, SHIFT, 1))
            held[part, 2 * ys + 1, zb] = jnp.where(lower, pltpu.roll(low, 16 - SHIFT, 1), high)
        leaving.append(pltpu.make_async_copy(held.at[part], out_ref.at[part], sems.at[xs]))
        leaving[-1].start()
    for copy in leaving:
        copy.wait()


def merge(regions, shape):
    paired = pair_shape(shape)
    nsx = slot_counts(shape)[0]
    volume = pl.pallas_call(
        lambda *refs: merge_kernel(shape, *refs),
        out_shape=jax.ShapeDtypeStruct(paired, jnp.bfloat16),
        in_specs=[pl.BlockSpec(memory_space=pltpu.VMEM)] * 8,
        out_specs=pl.BlockSpec(memory_space=pl.ANY),
        scratch_shapes=[pltpu.VMEM(paired, jnp.bfloat16), pltpu.SemaphoreType.DMA((nsx,))],
        name="merge",
    )(*regions)
    volume = volume.reshape(paired[0], paired[1], paired[2], 2, BLK, paired[4])
    return volume.transpose(0, 1, 3, 2, 4, 5).reshape(shape)


def dot(a, b):
    return lax.dot_general(a, b, (((1,), (0,)), ((), ())), preferred_element_type=jnp.float32)


def halves_of(value):
    high = value.astype(jnp.bfloat16)
    return high, (value - high.astype(jnp.float32)).astype(jnp.bfloat16)


def wide_dot(a, b):
    (ah, al), (bh, bl) = a, b
    return dot(ah, bh) + (dot(ah, bl) + dot(al, bh))


def shrink_kernel(shape, pass_index, offsets_ref, coefficients_ref, *refs):
    in_refs, out_refs, (held, result) = refs[:8], refs[8:16], refs[16:]
    nsx, nsy, nsz = slot_counts(shape)
    frames = shape[3]
    for at, region in enumerate(REGIONS):
        xsl, ysl, zsl = region_slices(region, shape)
        held[zsl, xsl, :, ysl] = in_refs[at][...]
    moved = [offsets_ref[pass_index, dim] // SHIFT for dim in range(3)]
    c0, c1, c2, c3, c4 = (coefficients_ref[degree] for degree in range(5))
    rows = lax.broadcasted_iota(jnp.int32, (frames, frames), 0)
    columns = lax.broadcasted_iota(jnp.int32, (frames, frames), 1)
    on_diagonal = rows == columns
    places = []
    for first in itertools.product(range(nsx // 2), range(nsy // 2), range(nsz // 2)):
        slots = [
            [lax.rem(2 * one + step + shift, count) for step in range(2)]
            for one, shift, count in zip(first, moved, (nsx, nsy, nsz))
        ]
        places.append(list(itertools.product(*slots)))

    def block_of(chunks):
        return jnp.concatenate([held[zs, xs, :, ys].reshape(SHIFT * 16, frames) for xs, ys, zs in chunks], 0)

    def gramian_of(block):
        return lax.dot_general(
            block, block, (((0,), (0,)), ((), ())), preferred_element_type=jnp.float32
        )

    def scale(gramian):
        diagonal = jnp.sum(jnp.where(on_diagonal, gramian, 0.0), 0, keepdims=True)
        trace = jnp.sum(diagonal, 1, keepdims=True)
        return gramian * (1.0 / (VOXB * (trace / (VOXB * frames) + 1e-6)))

    def squared(scaled):
        high, low = halves_of(scaled)
        cross = dot(high, low)
        return dot(high, high) + (cross + cross.T)

    def polynomial(scaled, square):
        inner = c4 * square + c3 * scaled + jnp.where(on_diagonal, c2, 0.0)
        poly = wide_dot(halves_of(inner), halves_of(square)) + c1 * scaled + jnp.where(on_diagonal, c0, 0.0)
        return poly.astype(jnp.bfloat16)

    scaled = [scale(one) for one in [gramian_of(block_of(chunks)) for chunks in places]]
    squares = [squared(one) for one in scaled]
    polys = [polynomial(one, square) for one, square in zip(scaled, squares)]
    for chunks, poly in zip(places, polys):
        rows_out = dot(block_of(chunks), poly).astype(jnp.bfloat16)
        for at, (xs, ys, zs) in enumerate(chunks):
            result[zs, xs, :, ys] = rows_out[64 * at : 64 * (at + 1)].reshape(SHIFT, 16, frames)
    for at, region in enumerate(REGIONS):
        xsl, ysl, zsl = region_slices(region, shape)
        out_refs[at][...] = result[zsl, xsl, :, ysl]


def shrink(regions, shape, pass_index, offsets, coefficients):
    nsx, nsy, nsz = slot_counts(shape)
    scratch = pltpu.VMEM((nsz, nsx, SHIFT, nsy, 16, shape[3]), jnp.bfloat16)
    whole = pl.BlockSpec(memory_space=pltpu.VMEM)
    scalars = pl.BlockSpec(memory_space=pltpu.SMEM)
    return pl.pallas_call(
        lambda *refs: shrink_kernel(shape, pass_index, *refs),
        out_shape=region_types(shape),
        in_specs=[scalars, scalars] + [whole] * 8,
        out_specs=[whole] * 8,
        scratch_shapes=[scratch, scratch],
        name=f"shrink{pass_index}",
    )(offsets, coefficients, *regions)


def sent(value, steps):
    sizes = [lax.axis_size(axis) for axis in AXES]
    steps = [step % size for step, size in zip(steps, sizes)]
    if not any(steps):
        return value
    pairs = []
    for source, at in enumerate(itertools.product(*(range(size) for size in sizes))):
        target = 0
        for place, step, size in zip(at, steps, sizes):
            target = target * size + (place + step) % size
        pairs.append((source, target))
    return lax.ppermute(value, AXES, pairs)


ORDER = ((0, 0, 1), (1, 0, 1), (0, 1, 1), (1, 1, 1), (1, 0, 0), (0, 1, 0), (1, 1, 0), (0, 0, 0))


def regroup(regions, index, radices, way):
    def branch(delta):
        def move(*held):
            return tuple(
                sent(one, [moves * step * (-1 if other else 1) for moves, step, other in zip(region, delta, MIRRORED)])
                for region, one in zip(ORDER, held[:7])
            ) + (lax.optimization_barrier(held[7]),)

        return move

    steps = [[way * (digit if digit < 2 else digit - radix) for digit in range(radix)] for radix in radices]
    branches = [branch(delta) for delta in itertools.product(*steps)]
    operands = tuple(regions[REGIONS.index(region)] for region in ORDER)
    moved = conditionals._switch_internal(index, branches, operands, branches_platforms=None)
    moved = dict(zip(ORDER, moved))
    return [moved[region] for region in REGIONS]


def local(volume, offsets, coefficients):
    shape = volume.shape
    two_way = [2 if lax.axis_size(axis) == 2 else 3 for axis in AXES]
    radices = [(2, 2, 2), two_way, (2, 2, 2)]
    regions, index, offsets, coefficients = split(volume, offsets, coefficients, radices)
    regions = regroup(regions, index[0], radices[0], -1)
    regions = shrink(regions, shape, 0, offsets, coefficients)
    regions = regroup(regions, index[1], radices[1], 1)
    regions = shrink(regions, shape, 1, offsets, coefficients)
    regions = regroup(regions, index[2], radices[2], 1)
    return merge(regions, shape)


def solution(mesh):
    return jax.shard_map(
        local,
        mesh=mesh,
        in_specs=(P("gx", "gy", "gz", None), P(), P()),
        out_specs=P("gx", "gy", "gz", None),
        check_vma=False,
    )
```
